32 devices in a mesh: coord: 8 (over z, y), cohort: 4 (over x, core).
Axes of the slice: x: 2, y: 2, z: 4, core: 2. Of those that a mesh axis runs over, the one named last changes fastest.
Arguments:
- shapes: bfloat16 [4, 1024, 32768], P('cohort', None, 'coord'), may hold values from -6 to 6
- sketch_signs: int32 [4, 1024, 128], P('cohort'), may hold values from -1 to 1
- merge_sketch: float32 [2, 2, 128, 128], replicated, may hold values from -1.5 to 1.5
Outputs:
- basis: float32 [4, 32768, 128], P('cohort', 'coord')
- scores: float32 [4, 1024, 128], P('cohort', 'coord')
The draws below stay inside these ranges and needn't reach their ends.
All inputs are finite; a program needn't handle non-finite values.
Results may differ from the reference program's by a relative error of at most 0.0086.
Values sent between devices are 32-bit elements; how exact they have to be, the bound alone decides.
A program may use at most 64 MiB of HBM per device.

```python
import math
import jax
import jax.numpy as jnp
from jax import lax

K = 128
SUBJ = 1024
LEVELS = 2
P_SIZE = 32768
COHORTS = 4


def draw_shapes(key, part):
    mode_key = jax.random.fold_in(key, 11)
    own_key = jax.random.fold_in(key, 12)
    coef_key = jax.random.fold_in(key, 13)
    noise_key = jax.random.fold_in(key, 14)
    modes = jax.random.normal(mode_key, (K, P_SIZE), jnp.float32)
    spread = 0.3 * jnp.power(0.97, jnp.arange(K, dtype=jnp.float32))
    coefs = jax.random.normal(coef_key, (COHORTS, SUBJ, K), jnp.float32) * spread
    own = jax.random.normal(own_key, (COHORTS, K, P_SIZE), jnp.float32)
    cohort_modes = modes[None] + 0.2 * own
    signal = jnp.einsum('csk,ckp->csp', coefs, cohort_modes)
    noise = 0.3 * jax.random.normal(noise_key, (COHORTS, SUBJ, P_SIZE), jnp.float32)
    values = signal + noise
    return jnp.clip(values, -6.0, 6.0).astype(jnp.bfloat16)


def draw_merge_sketch(key, part):
    mix_key = jax.random.fold_in(key, 21)
    noise = jnp.clip(jax.random.normal(mix_key, (LEVELS, 2, K, K), jnp.float32), -6.0, 6.0)
    noise = noise * (0.2 * K ** (-0.5))
    ident = jnp.eye(K, dtype=jnp.float32)
    lower_map = ident[None] + noise[:, 0]
    upper_map = noise[:, 1]
    return jnp.stack([lower_map, upper_map], axis=1)


def set_ends(entries, key, smallest, top_value):
    longest = entries.shape.index(max(entries.shape))
    spots = []
    for shift in (0, 1):
        where = [jax.random.randint(jax.random.fold_in(key, axis), (), 0, length) for axis, length in enumerate(entries.shape)]
        where[longest] = (where[longest] + shift) % entries.shape[longest]
        spots.append(tuple(where))
    return entries.at[spots[0]].set(smallest).at[spots[1]].set(top_value)


def setup_inputs(seed: int = 0) -> dict:
    splits = jax.random.split(jax.random.key(seed), 4)
    return {
        "shapes": draw_shapes(jax.random.fold_in(splits[3], 71), 0),
        "sketch_signs": set_ends(jax.random.randint(splits[1], (COHORTS, SUBJ, K), -1, 2), jax.random.fold_in(splits[1], 1), -1, 1).astype(jnp.int32),
        "merge_sketch": draw_merge_sketch(jax.random.fold_in(splits[3], 71), 0),
    }


def lower_inverse_t(gram):
    factor = jnp.linalg.cholesky(gram)
    ident = jnp.eye(gram.shape[0], dtype=gram.dtype)
    inverse = jax.scipy.linalg.solve_triangular(factor, ident, lower=True)
    return inverse.T

def orthonormal(mixed):
    gram = jnp.dot(mixed.T, mixed, precision=lax.Precision.HIGHEST)
    return jnp.dot(mixed, lower_inverse_t(gram), precision=lax.Precision.HIGHEST)

def reference(shapes, sketch_signs, merge_sketch):
    count = shapes.shape[0]
    centered_all = []
    bases = []
    for cohort in range(count):
        data = shapes[cohort].astype(jnp.float32)
        centered = (data - lax.optimization_barrier(jnp.mean(data, axis=0, keepdims=True))).astype(jnp.bfloat16)
        centered_all.append(centered)
        signs = sketch_signs[cohort].astype(jnp.bfloat16)
        sketch = jnp.dot(centered.T.astype(jnp.float32), signs.astype(jnp.float32), preferred_element_type=jnp.float32)
        bases.append(orthonormal(sketch))
    for level in range(LEVELS):
        merged = []
        for cohort in range(count):
            lower = cohort & ~(1 << level)
            upper = lower | 1 << level
            mixed = jnp.dot(bases[lower], merge_sketch[level, 0], precision=lax.Precision.HIGHEST)
            mixed = mixed + jnp.dot(bases[upper], merge_sketch[level, 1], precision=lax.Precision.HIGHEST)
            merged.append(orthonormal(mixed))
        bases = merged
    factor = 4.0 * math.sqrt(K / P_SIZE)
    basis_out = jnp.stack([b * math.sqrt(P_SIZE) for b in bases])
    score_out = jnp.stack([jnp.dot(centered_all[c].astype(jnp.float32), bases[c].astype(jnp.bfloat16).astype(jnp.float32), preferred_element_type=jnp.float32) * factor for c in range(count)])
    return (basis_out, score_out)
```

```python
import functools
import math

import jax
import jax.numpy as jnp
from jax import lax
from jax.experimental import pallas as pl
from jax.experimental.pallas import tpu as pltpu
from jax.sharding import PartitionSpec as P

LEVELS = 2
HIGHEST = lax.Precision.HIGHEST
MESH = pl.DeviceIdType.MESH
VMEM = pl.BlockSpec(memory_space=pltpu.VMEM)


def peers_of(n, pair):
    coord = lax.axis_index("coord")
    if not pair:
        return coord, n, lambda rank: {"coord": rank}
    cohort = lax.axis_index("cohort")
    side = lax.rem(cohort, 2)
    base = cohort - side
    rank = coord * 2 + side
    return rank, 2 * n, lambda r: {"coord": r // 2, "cohort": base + lax.rem(r, 2)}


def enter(me, size, ident):
    barrier = pltpu.get_barrier_semaphore()
    for d in range(1, size):
        pl.semaphore_signal(
            barrier, inc=1, device_id=ident(lax.rem(me + d, size)), device_id_type=MESH
        )
    pl.semaphore_wait(barrier, size - 1)


def scatter_sum(part_ref, recv, me, size, ident, send, got):
    copies = []
    for d in range(1, size):
        peer = lax.rem(me + d, size)
        copies.append(
            pltpu.make_async_remote_copy(
                src_ref=part_ref.at[peer],
                dst_ref=recv.at[d],
                send_sem=send.at[d],
                recv_sem=got.at[d],
                device_id=ident(peer),
                device_id_type=MESH,
            )
        )
    for copy in copies:
        copy.start()
    total = part_ref[me]
    for d in range(1, size):
        copies[d - 1].wait_recv()
        total = total + recv[d]
    return total, copies


def all_sum_kernel(n, pair, part_ref, out_ref, recv, send, got, send2, got2):
    me, size, ident = peers_of(n, pair)
    enter(me, size, ident)
    total, copies = scatter_sum(part_ref, recv, me, size, ident, send, got)
    out_ref[me] = total
    spread = []
    for d in range(1, size):
        spread.append(
            pltpu.make_async_remote_copy(
                src_ref=out_ref.at[me],
                dst_ref=out_ref.at[me],
                send_sem=send2.at[d],
                recv_sem=got2.at[d],
                device_id=ident(lax.rem(me + d, size)),
                device_id_type=MESH,
            )
        )
    for copy in spread:
        copy.start()
    for copy in spread:
        copy.wait_recv()
    for copy in copies + spread:
        copy.wait_send()


def all_sum(part, n, pair, ident):
    size = 2 * n if pair else n
    rows, cols = part.shape
    shape = (size, rows // size, cols)
    out = pl.pallas_call(
        functools.partial(all_sum_kernel, n, pair),
        out_shape=jax.ShapeDtypeStruct(shape, part.dtype),
        in_specs=[VMEM],
        out_specs=VMEM,
        scratch_shapes=[pltpu.VMEM(shape, part.dtype)] + [pltpu.SemaphoreType.DMA((size,))] * 4,
        compiler_params=pltpu.CompilerParams(collective_id=ident, has_side_effects=True),
        name=f"all_sum_{ident}",
    )(part.reshape(shape))
    return out.reshape(rows, cols)


def score_kernel(n, scale, part_ref, out_ref, recv, send, got):
    me, size, ident = peers_of(n, False)
    enter(me, size, ident)
    total, copies = scatter_sum(part_ref, recv, me, size, ident, send, got)
    out_ref[...] = total * scale
    for copy in copies:
        copy.wait_send()


def score_sum(part, n, scale, ident):
    rows, cols = part.shape
    shape = (n, rows // n, cols)
    return pl.pallas_call(
        functools.partial(score_kernel, n, scale),
        out_shape=jax.ShapeDtypeStruct(shape[1:], part.dtype),
        in_specs=[VMEM],
        out_specs=VMEM,
        scratch_shapes=[pltpu.VMEM(shape, part.dtype)] + [pltpu.SemaphoreType.DMA((n,))] * 2,
        compiler_params=pltpu.CompilerParams(collective_id=ident, has_side_effects=True),
        name="score_sum",
    )(part.reshape(shape))


def inverse_kernel(g_ref, x_ref):
    size = g_ref.shape[0]
    step = 8
    tiles = size // step
    lane = lax.broadcasted_iota(jnp.int32, (step, size), 1)
    sub = lax.broadcasted_iota(jnp.int32, (step, size), 0)
    left = [g_ref[t * step : (t + 1) * step, :] for t in range(tiles)]
    right = [(lane == sub + t * step).astype(jnp.float32) for t in range(tiles)]
    for t in range(tiles):
        pivots = jnp.ones((step, size), jnp.float32)
        for s in range(step):
            j = t * step + s
            row = jnp.broadcast_to(left[t][s : s + 1, :], (step, size))
            row_x = jnp.broadcast_to(right[t][s : s + 1, :], (step, size))
            pivot = jnp.broadcast_to(row[:, j : j + 1], (step, size))
            pivots = jnp.where(sub == s, pivot, pivots)
            inv = 1.0 / pivot
            for u in range(t, tiles):
                if u == t and s == step - 1:
                    continue
                factor = jnp.broadcast_to(left[u][:, j : j + 1], (step, size)) * inv
                if u == t:
                    factor = jnp.where(sub > s, factor, 0.0)
                left[u] = left[u] - factor * row
                right[u] = right[u] - factor * row_x
        x_ref[t * step : (t + 1) * step, :] = right[t] * lax.rsqrt(pivots)


def lower_inverse(gram):
    return pl.pallas_call(
        inverse_kernel,
        out_shape=jax.ShapeDtypeStruct(gram.shape, gram.dtype),
        in_specs=[VMEM],
        out_specs=VMEM,
        name="lower_inverse",
    )(gram)


def gram_of(rows):
    return lax.dot_general(rows, rows, (((0,), (0,)), ((), ())), precision=HIGHEST)


def times_t(a, b):
    return lax.dot_general(a, b, (((1,), (1,)), ((), ())), precision=HIGHEST)


def swap(value, distance):
    size = lax.axis_size("cohort")
    return lax.ppermute(value, "cohort", [(i, i ^ distance) for i in range(size)])


def on_device(shapes, sketch_signs, merge_sketch):
    n = lax.axis_size("coord")
    data = shapes[0].astype(jnp.float32)
    centered = (data - jnp.mean(data, axis=0, keepdims=True)).astype(jnp.bfloat16)
    signs = sketch_signs[0].astype(jnp.bfloat16)
    sketch = lax.dot_general(
        centered, signs, (((0,), (0,)), ((), ())), preferred_element_type=jnp.float32
    )
    position = lax.axis_index("cohort")
    side = position % 2
    upper = position >> 1 & 1 == 1

    own = times_t(sketch, lower_inverse(all_sum(gram_of(sketch), n, False, 0)))
    partner = swap(own, 1)
    lower_basis = jnp.where(side == 1, partner, own)
    upper_basis = jnp.where(side == 1, own, partner)
    mixed = jnp.matmul(lower_basis, merge_sketch[0, 0], precision=HIGHEST)
    mixed = mixed + jnp.matmul(upper_basis, merge_sketch[0, 1], precision=HIGHEST)

    half = mixed.shape[0] // 2
    mine = lax.dynamic_slice_in_dim(mixed, side * half, half, 0)
    theirs = swap(mine, 2)
    inverse = lower_inverse(all_sum(gram_of(mixed), n, False, 1))
    inverse_other = swap(inverse, 2)
    low_map = lax.dot_general(
        jnp.where(upper, inverse_other, inverse),
        merge_sketch[1, 0],
        (((0,), (0,)), ((), ())),
        precision=HIGHEST,
    )
    high_map = lax.dot_general(
        jnp.where(upper, inverse, inverse_other),
        merge_sketch[1, 1],
        (((0,), (0,)), ((), ())),
        precision=HIGHEST,
    )
    own_map = jnp.where(upper, high_map, low_map)
    other_map = jnp.where(upper, low_map, high_map)
    merged = jnp.matmul(mine, own_map, precision=HIGHEST)
    merged = merged + jnp.matmul(theirs, other_map, precision=HIGHEST)
    own_half = times_t(merged, lower_inverse(all_sum(gram_of(merged), n, True, 2)))
    other_half = swap(own_half, 1)
    first = jnp.where(side == 1, other_half, own_half)
    second = jnp.where(side == 1, own_half, other_half)
    current = jnp.concatenate([first, second], axis=0)

    width = current.shape[1]
    total_coords = current.shape[0] * n
    rounded = current.astype(jnp.bfloat16)
    partial = jnp.dot(centered, rounded, preferred_element_type=jnp.float32)
    scores = score_sum(partial, n, 4.0 * math.sqrt(width / total_coords), 3)
    basis_out = current * math.sqrt(total_coords)
    return (basis_out[None], scores[None])


def solution(mesh):
    placed = (P("cohort", None, "coord"), P("cohort", None, None), P())
    return jax.shard_map(
        on_device,
        mesh=mesh,
        in_specs=placed,
        out_specs=(P("cohort", "coord", None), P("cohort", "coord", None)),
        check_vma=False,
    )
```

```python
import functools
import math

import jax
import jax.numpy as jnp
from jax import lax
from jax.experimental import pallas as pl
from jax.experimental.pallas import tpu as pltpu
from jax.sharding import PartitionSpec as P

LEVELS = 2
HIGHEST = lax.Precision.HIGHEST
MESH = pl.DeviceIdType.MESH
VMEM = pl.BlockSpec(memory_space=pltpu.VMEM)


def peers_of(n, pair):
    coord = lax.axis_index("coord")
    if not pair:
        return coord, n, lambda rank: {"coord": rank}
    cohort = lax.axis_index("cohort")
    side = lax.rem(cohort, 2)
    base = cohort - side
    rank = coord * 2 + side
    return rank, 2 * n, lambda r: {"coord": r // 2, "cohort": base + lax.rem(r, 2)}


def enter(me, size, ident):
    barrier = pltpu.get_barrier_semaphore()
    for d in range(1, size):
        pl.semaphore_signal(
            barrier, inc=1, device_id=ident(lax.rem(me + d, size)), device_id_type=MESH
        )
    pl.semaphore_wait(barrier, size - 1)


def scatter_sum(part_ref, recv, me, size, ident, send, got):
    copies = []
    for d in range(1, size):
        peer = lax.rem(me + d, size)
        copies.append(
            pltpu.make_async_remote_copy(
                src_ref=part_ref.at[peer],
                dst_ref=recv.at[d],
                send_sem=send.at[d],
                recv_sem=got.at[d],
                device_id=ident(peer),
                device_id_type=MESH,
            )
        )
    for copy in copies:
        copy.start()
    total = part_ref[me]
    for d in range(1, size):
        copies[d - 1].wait_recv()
        total = total + recv[d]
    return total, copies


def all_sum_kernel(n, pair, part_ref, out_ref, recv, send, got, send2, got2):
    me, size, ident = peers_of(n, pair)
    enter(me, size, ident)
    total, copies = scatter_sum(part_ref, recv, me, size, ident, send, got)
    out_ref[me] = total
    spread = []
    for d in range(1, size):
        spread.append(
            pltpu.make_async_remote_copy(
                src_ref=out_ref.at[me],
                dst_ref=out_ref.at[me],
                send_sem=send2.at[d],
                recv_sem=got2.at[d],
                device_id=ident(lax.rem(me + d, size)),
                device_id_type=MESH,
            )
        )
    for copy in spread:
        copy.start()
    for copy in spread:
        copy.wait_recv()
    for copy in copies + spread:
        copy.wait_send()


def all_sum(part, n, pair, ident):
    size = 2 * n if pair else n
    rows, cols = part.shape
    shape = (size, rows // size, cols)
    out = pl.pallas_call(
        functools.partial(all_sum_kernel, n, pair),
        out_shape=jax.ShapeDtypeStruct(shape, part.dtype),
        in_specs=[VMEM],
        out_specs=VMEM,
        scratch_shapes=[pltpu.VMEM(shape, part.dtype)] + [pltpu.SemaphoreType.DMA((size,))] * 4,
        compiler_params=pltpu.CompilerParams(collective_id=ident, has_side_effects=True),
        name=f"all_sum_{ident}",
    )(part.reshape(shape))
    return out.reshape(rows, cols)


def score_kernel(n, scale, part_ref, out_ref, recv, send, got):
    me, size, ident = peers_of(n, False)
    enter(me, size, ident)
    total, copies = scatter_sum(part_ref, recv, me, size, ident, send, got)
    out_ref[...] = total * scale
    for copy in copies:
        copy.wait_send()


def score_sum(part, n, scale, ident):
    rows, cols = part.shape
    shape = (n, rows // n, cols)
    return pl.pallas_call(
        functools.partial(score_kernel, n, scale),
        out_shape=jax.ShapeDtypeStruct(shape[1:], part.dtype),
        in_specs=[VMEM],
        out_specs=VMEM,
        scratch_shapes=[pltpu.VMEM(shape, part.dtype)] + [pltpu.SemaphoreType.DMA((n,))] * 2,
        compiler_params=pltpu.CompilerParams(collective_id=ident, has_side_effects=True),
        name="score_sum",
    )(part.reshape(shape))


def inverse_of(g_ref, x_ref):
    size = g_ref.shape[0]
    step = 8
    tiles = size // step
    lane = lax.broadcasted_iota(jnp.int32, (step, size), 1)
    sub = lax.broadcasted_iota(jnp.int32, (step, size), 0)

    def full(x):
        return jnp.broadcast_to(x, (step, size))

    def total(terms):
        while len(terms) > 1:
            terms = [terms[i] + terms[i + 1] for i in range(0, len(terms), 2)]
        return terms[0]

    left = [g_ref[t * step : (t + 1) * step, :] for t in range(tiles)]
    right = [(lane == sub + t * step).astype(jnp.float32) for t in range(tiles)]
    for t in range(tiles):
        at = t * step
        cols = [full(left[t][:, at + k : at + k + 1]) for k in range(step)]
        e = [[full(cols[k][i : i + 1, :]) for k in range(i + 1)] for i in range(step)]
        rows = [full(left[t][i : i + 1, :]) for i in range(step)]
        rows_x = [full(right[t][i : i + 1, :]) for i in range(step)]
        f = {}
        inv = []
        for s in range(step):
            inv.append(1.0 / e[s][s])
            for i in range(s + 1, step):
                f[i, s] = e[i][s] * inv[s]
                for k in range(s + 1, i + 1):
                    e[i][k] = e[i][k] - f[i, s] * e[k][s]
            for i in range(s + 1, step):
                rows[i] = rows[i] - f[i, s] * rows[s]
                rows_x[i] = rows_x[i] - f[i, s] * rows_x[s]
        out = rows_x[0] * lax.rsqrt(e[0][0])
        for s in range(1, step):
            out = jnp.where(sub == s, rows_x[s] * lax.rsqrt(e[s][s]), out)
        x_ref[at : at + step, :] = out
        rows = [rows[s] * inv[s] for s in range(step)]
        rows_x = [rows_x[s] * inv[s] for s in range(step)]
        for u in range(t + 1, tiles):
            c = [full(left[u][:, at + s : at + s + 1]) for s in range(step)]
            for s in range(step):
                for r in range(s):
                    c[s] = c[s] - f[s, r] * c[r]
            left[u] = left[u] - total([c[s] * rows[s] for s in range(step)])
            right[u] = right[u] - total([c[s] * rows_x[s] for s in range(step)])


def map_kernel(g_ref, mix_ref, out_ref, x_ref):
    inverse_of(g_ref, x_ref)
    out_ref[...] = lax.dot_general(
        x_ref[...],
        mix_ref[...],
        (((0,), (0,)), ((), ())),
        precision=HIGHEST,
        preferred_element_type=jnp.float32,
    )


def lower_inverse(gram):
    return pl.pallas_call(
        inverse_of,
        out_shape=jax.ShapeDtypeStruct(gram.shape, gram.dtype),
        in_specs=[VMEM],
        out_specs=VMEM,
        name="lower_inverse",
    )(gram)


def mixing_map(gram, mix):
    return pl.pallas_call(
        map_kernel,
        out_shape=jax.ShapeDtypeStruct(gram.shape, gram.dtype),
        in_specs=[VMEM, VMEM],
        out_specs=VMEM,
        scratch_shapes=[pltpu.VMEM(gram.shape, gram.dtype)],
        name="mixing_map",
    )(gram, mix)


def sketch_kernel(shapes_ref, signs_ref, centered_ref, sketch_ref, turned):
    @pl.when(pl.program_id(0) == 0)
    def _():
        turned[...] = signs_ref[...].astype(jnp.float32).T.astype(jnp.bfloat16)

    data = shapes_ref[...].astype(jnp.float32)
    mean = jnp.sum(data, axis=0, keepdims=True) * (1.0 / data.shape[0])
    centered = (data - mean).astype(jnp.bfloat16)
    centered_ref[...] = centered
    sketch_ref[...] = jnp.dot(turned[...], centered, preferred_element_type=jnp.float32).T


def center_and_sketch(shapes, signs):
    subjects, coords = shapes.shape
    width = signs.shape[1]
    tile = math.gcd(coords, 512)
    return pl.pallas_call(
        sketch_kernel,
        grid=(coords // tile,),
        out_shape=(
            jax.ShapeDtypeStruct((subjects, coords), jnp.bfloat16),
            jax.ShapeDtypeStruct((coords, width), jnp.float32),
        ),
        in_specs=[
            pl.BlockSpec((subjects, tile), lambda i: (0, i)),
            pl.BlockSpec((subjects, width), lambda i: (0, 0)),
        ],
        out_specs=(
            pl.BlockSpec((subjects, tile), lambda i: (0, i)),
            pl.BlockSpec((tile, width), lambda i: (i, 0)),
        ),
        scratch_shapes=[pltpu.VMEM((width, subjects), jnp.bfloat16)],
        name="center_and_sketch",
    )(shapes, signs)


def project_kernel(side_ref, centered_ref, basis_ref, *rest):
    out_ref = rest[-1]

    @pl.when(pl.program_id(0) == 0)
    def _():
        out_ref[...] = rest[0][...] if len(rest) > 1 else jnp.zeros_like(out_ref)

    out_ref[...] += jnp.dot(
        centered_ref[...], basis_ref[...].astype(jnp.bfloat16), preferred_element_type=jnp.float32
    )


def project(side, centered, basis, start=None):
    subjects = centered.shape[0]
    half, width = basis.shape
    tile = math.gcd(half, 1024)
    steps = half // tile
    extra = [] if start is None else [start]
    whole = pl.BlockSpec((subjects, width), lambda i, side: (0, 0))
    return pl.pallas_call(
        project_kernel,
        grid_spec=pltpu.PrefetchScalarGridSpec(
            num_scalar_prefetch=1,
            grid=(steps,),
            in_specs=[
                pl.BlockSpec((subjects, tile), lambda i, side: (0, side[0] * steps + i)),
                pl.BlockSpec((tile, width), lambda i, side: (i, 0)),
            ]
            + [whole] * len(extra),
            out_specs=whole,
        ),
        out_shape=jax.ShapeDtypeStruct((subjects, width), jnp.float32),
        cost_estimate=pl.CostEstimate(
            flops=2 * subjects * half * width, bytes_accessed=2 * subjects * half, transcendentals=0
        ),
        name="project",
    )(side.reshape(1), centered, basis, *extra)


def gram_of(rows):
    return lax.dot_general(rows, rows, (((0,), (0,)), ((), ())), precision=HIGHEST)


def times_t(a, b):
    return lax.dot_general(a, b, (((1,), (1,)), ((), ())), precision=HIGHEST)


def mix(own, own_map, other, other_map):
    return jnp.matmul(own, own_map, precision=HIGHEST) + jnp.matmul(
        other, other_map, precision=HIGHEST
    )


def swap(value, distance):
    size = lax.axis_size("cohort")
    return lax.ppermute(value, "cohort", [(i, i ^ distance) for i in range(size)])


def on_device(shapes, sketch_signs, merge_sketch):
    n = lax.axis_size("coord")
    position = lax.axis_index("cohort")
    side = position % 2
    upper = position // 2 % 2
    centered, sketch = center_and_sketch(shapes[0], sketch_signs[0])

    half = sketch.shape[0] // 2
    mine = lax.dynamic_slice_in_dim(sketch, side * half, half, 0)
    theirs = swap(lax.dynamic_slice_in_dim(sketch, (1 - side) * half, half, 0), 1)
    own_map = mixing_map(all_sum(gram_of(sketch), n, False, 0), merge_sketch[0][side])
    mine = mix(mine, own_map, theirs, swap(own_map, 1))

    theirs = swap(mine, 2)
    own_map = mixing_map(all_sum(gram_of(mine), n, True, 1), merge_sketch[1][upper])
    mine = mix(mine, own_map, theirs, swap(own_map, 2))

    own_half = times_t(mine, lower_inverse(all_sum(gram_of(mine), n, True, 2)))
    other_half = swap(own_half, 1)
    partial = project(side, centered, own_half)
    partial = project(1 - side, centered, other_half, partial)
    first = jnp.where(side == 1, other_half, own_half)
    second = jnp.where(side == 1, own_half, other_half)
    current = jnp.concatenate([first, second], axis=0)

    width = current.shape[1]
    total_coords = current.shape[0] * n
    scores = score_sum(partial, n, 4.0 * math.sqrt(width / total_coords), 3)
    basis_out = current * math.sqrt(total_coords)
    return (basis_out[None], scores[None])


def solution(mesh):
    placed = (P("cohort", None, "coord"), P("cohort", None, None), P())
    return jax.shard_map(
        on_device,
        mesh=mesh,
        in_specs=placed,
        out_specs=(P("cohort", "coord", None), P("cohort", "coord", None)),
        check_vma=False,
    )
```

```python
import functools
import math

import jax
import jax.numpy as jnp
from jax import lax
from jax.experimental import pallas as pl
from jax.experimental.pallas import tpu as pltpu
from jax.sharding import PartitionSpec as P

LEVELS = 2
HIGHEST = lax.Precision.HIGHEST
MESH = pl.DeviceIdType.MESH
VMEM = pl.BlockSpec(memory_space=pltpu.VMEM)


def peers_of(n, pair):
    coord = lax.axis_index("coord")
    if not pair:
        return coord, n, lambda rank: {"coord": rank}
    cohort = lax.axis_index("cohort")
    side = lax.rem(cohort, 2)
    base = cohort - side
    rank = coord * 2 + side
    return rank, 2 * n, lambda r: {"coord": r // 2, "cohort": base + lax.rem(r, 2)}


def greet(me, size, ident):
    barrier = pltpu.get_barrier_semaphore()
    for d in range(1, size):
        pl.semaphore_signal(
            barrier, inc=1, device_id=ident(lax.rem(me + d, size)), device_id_type=MESH
        )
    return barrier


def send_block(part_ref, recv, me, size, ident, send, got, d):
    peer = lax.rem(me + d, size)
    return pltpu.make_async_remote_copy(
        src_ref=part_ref.at[peer],
        dst_ref=recv.at[d],
        send_sem=send.at[d],
        recv_sem=got.at[d],
        device_id=ident(peer),
        device_id_type=MESH,
    )


def gram_sum_kernel(n, pair, count, *refs):
    rows_refs, (out_ref, gram, part, recv, send, got, send2, got2) = refs[:count], refs[count:]
    me, size, ident = peers_of(n, pair)
    barrier = greet(me, size, ident)
    block = part.shape[1]
    gram[...] = jnp.zeros_like(gram)
    for rows_ref in rows_refs:
        step = math.gcd(rows_ref.shape[0], 512)

        def add(i, carry, rows_ref=rows_ref, step=step):
            rows = rows_ref[pl.ds(pl.multiple_of(i * step, step), step), :]
            gram[...] += lax.dot_general(
                rows,
                rows,
                (((0,), (0,)), ((), ())),
                precision=HIGHEST,
                preferred_element_type=jnp.float32,
            )
            return carry

        lax.fori_loop(0, rows_ref.shape[0] // step, add, 0)
    for r in range(size):
        part[r] = gram[r * block : (r + 1) * block, :]
    pl.semaphore_wait(barrier, size - 1)
    copies = [send_block(part, recv, me, size, ident, send, got, d) for d in range(1, size)]
    for copy in copies:
        copy.start()
    total = part[me]
    for d in range(1, size):
        copies[d - 1].wait_recv()
        total = total + recv[d]
    out_ref[me] = total
    spread = []
    for d in range(1, size):
        spread.append(
            pltpu.make_async_remote_copy(
                src_ref=out_ref.at[me],
                dst_ref=out_ref.at[me],
                send_sem=send2.at[d],
                recv_sem=got2.at[d],
                device_id=ident(lax.rem(me + d, size)),
                device_id_type=MESH,
            )
        )
    for copy in spread:
        copy.start()
    for copy in spread:
        copy.wait_recv()
    for copy in copies + spread:
        copy.wait_send()


def gram_sum(parts, n, pair, ident):
    size = 2 * n if pair else n
    width = parts[0].shape[1]
    dtype = parts[0].dtype
    shape = (size, width // size, width)
    out = pl.pallas_call(
        functools.partial(gram_sum_kernel, n, pair, len(parts)),
        out_shape=jax.ShapeDtypeStruct(shape, dtype),
        in_specs=[VMEM] * len(parts),
        out_specs=VMEM,
        scratch_shapes=[
            pltpu.VMEM((width, width), dtype),
            pltpu.VMEM(shape, dtype),
            pltpu.VMEM(shape, dtype),
        ]
        + [pltpu.SemaphoreType.DMA((size,))] * 4,
        compiler_params=pltpu.CompilerParams(collective_id=ident, has_side_effects=True),
        name=f"gram_sum_{ident}",
    )(*parts)
    return out.reshape(width, width)


def score_kernel(
    n, scale, centered_ref, own_ref, basis_ref, out_ref,
    held, narrow, part, recv, loaded, send, got, swap_send, swap_got,
):
    me, size, ident = peers_of(n, False)
    cohort = lax.axis_index("cohort")
    side = lax.rem(cohort, 2)
    partner = {"cohort": cohort + 1 - 2 * side}
    rows, half = held.shape[2:]
    order = [lax.rem(me + d, size) for d in list(range(1, size)) + [0]]
    loads = []
    for peer in order:
        pair = []
        for h in range(2):
            pair.append(
                pltpu.make_async_copy(
                    centered_ref.at[
                        pl.ds(pl.multiple_of(peer * rows, rows), rows), pl.ds(h * half, half)
                    ],
                    held.at[peer, h],
                    loaded.at[peer, h],
                )
            )
        loads.append(pair)
        for copy in pair:
            copy.start()
    barrier = greet(me, size, ident)
    pl.semaphore_signal(barrier, inc=1, device_id=partner, device_id_type=MESH)
    basis_ref[side] = own_ref[...]
    narrow[...] = own_ref[...].astype(jnp.bfloat16)
    pl.semaphore_wait(barrier, size)
    cross = pltpu.make_async_remote_copy(
        src_ref=own_ref,
        dst_ref=basis_ref.at[side],
        send_sem=swap_send,
        recv_sem=swap_got,
        device_id=partner,
        device_id_type=MESH,
    )
    cross.start()
    for peer, pair in zip(order, loads):
        for copy in pair:
            copy.wait()
        part[peer] = jnp.dot(held[peer, side], narrow[...], preferred_element_type=jnp.float32)
    cross.wait_recv()
    narrow[...] = basis_ref[1 - side].astype(jnp.bfloat16)
    copies = []
    for d, peer in zip(list(range(1, size)) + [0], order):
        part[peer] = part[peer] + jnp.dot(
            held[peer, 1 - side], narrow[...], preferred_element_type=jnp.float32
        )
        if d:
            copies.append(send_block(part, recv, me, size, ident, send, got, d))
            copies[-1].start()
    total = part[me]
    for d in range(1, size):
        copies[d - 1].wait_recv()
        total = total + recv[d]
    out_ref[...] = total * scale
    cross.wait_send()
    for copy in copies:
        copy.wait_send()


def basis_and_scores(centered, own, n, scale, ident):
    subjects = centered.shape[0]
    half, width = own.shape
    rows = subjects // n
    blocks = (n, rows, width)
    basis, scores = pl.pallas_call(
        functools.partial(score_kernel, n, scale),
        out_shape=(
            jax.ShapeDtypeStruct((2, half, width), own.dtype),
            jax.ShapeDtypeStruct((rows, width), jnp.float32),
        ),
        in_specs=[pl.BlockSpec(memory_space=pl.ANY), VMEM],
        out_specs=(VMEM, VMEM),
        scratch_shapes=[
            pltpu.VMEM((n, 2, rows, half), centered.dtype),
            pltpu.VMEM((half, width), jnp.bfloat16),
            pltpu.VMEM(blocks, jnp.float32),
            pltpu.VMEM(blocks, jnp.float32),
            pltpu.SemaphoreType.DMA((n, 2)),
            pltpu.SemaphoreType.DMA((n,)),
            pltpu.SemaphoreType.DMA((n,)),
            pltpu.SemaphoreType.DMA,
            pltpu.SemaphoreType.DMA,
        ],
        compiler_params=pltpu.CompilerParams(collective_id=ident, has_side_effects=True),
        name="basis_and_scores",
    )(centered, own)
    return basis.reshape(2 * half, width), scores


def inverse_of(g_ref, x_ref):
    size = g_ref.shape[0]
    step = 8
    tiles = size // step
    lane = lax.broadcasted_iota(jnp.int32, (step, size), 1)
    sub = lax.broadcasted_iota(jnp.int32, (step, size), 0)

    def full(x):
        return jnp.broadcast_to(x, (step, size))

    def total(terms):
        while len(terms) > 1:
            terms = [terms[i] + terms[i + 1] for i in range(0, len(terms), 2)]
        return terms[0]

    left = [g_ref[t * step : (t + 1) * step, :] for t in range(tiles)]
    right = [(lane == sub + t * step).astype(jnp.float32) for t in range(tiles)]
    for t in range(tiles):
        at = t * step
        cols = [full(left[t][:, at + k : at + k + 1]) for k in range(step)]
        e = [[full(cols[k][i : i + 1, :]) for k in range(i + 1)] for i in range(step)]
        rows = [full(left[t][i : i + 1, :]) for i in range(step)]
        rows_x = [full(right[t][i : i + 1, :]) for i in range(step)]
        f = {}
        inv = []
        for s in range(step):
            inv.append(1.0 / e[s][s])
            for i in range(s + 1, step):
                f[i, s] = e[i][s] * inv[s]
                for k in range(s + 1, i + 1):
                    e[i][k] = e[i][k] - f[i, s] * e[k][s]
            for i in range(s + 1, step):
                rows[i] = rows[i] - f[i, s] * rows[s]
                rows_x[i] = rows_x[i] - f[i, s] * rows_x[s]
        out = rows_x[0] * lax.rsqrt(e[0][0])
        for s in range(1, step):
            out = jnp.where(sub == s, rows_x[s] * lax.rsqrt(e[s][s]), out)
        x_ref[at : at + step, :] = out
        rows = [rows[s] * inv[s] for s in range(step)]
        rows_x = [rows_x[s] * inv[s] for s in range(step)]
        for u in range(t + 1, tiles):
            c = [full(left[u][:, at + s : at + s + 1]) for s in range(step)]
            for s in range(step):
                for r in range(s):
                    c[s] = c[s] - f[s, r] * c[r]
            left[u] = left[u] - total([c[s] * rows[s] for s in range(step)])
            right[u] = right[u] - total([c[s] * rows_x[s] for s in range(step)])


def map_kernel(g_ref, mix_ref, out_ref, x_ref):
    inverse_of(g_ref, x_ref)
    out_ref[...] = lax.dot_general(
        x_ref[...],
        mix_ref[...],
        (((0,), (0,)), ((), ())),
        precision=HIGHEST,
        preferred_element_type=jnp.float32,
    )


def lower_inverse(gram):
    return pl.pallas_call(
        inverse_of,
        out_shape=jax.ShapeDtypeStruct(gram.shape, gram.dtype),
        in_specs=[VMEM],
        out_specs=VMEM,
        name="lower_inverse",
    )(gram)


def mixing_map(gram, mix):
    return pl.pallas_call(
        map_kernel,
        out_shape=jax.ShapeDtypeStruct(gram.shape, gram.dtype),
        in_specs=[VMEM, VMEM],
        out_specs=VMEM,
        scratch_shapes=[pltpu.VMEM(gram.shape, gram.dtype)],
        name="mixing_map",
    )(gram, mix)


def sketch_kernel(steps, side_ref, shapes_ref, signs_ref, centered_ref, mine_ref, given_ref, turned):
    i = pl.program_id(0)

    @pl.when(i == 0)
    def _():
        turned[...] = signs_ref[...].astype(jnp.float32).T.astype(jnp.bfloat16)

    data = shapes_ref[...].astype(jnp.float32)
    mean = jnp.sum(data, axis=0, keepdims=True) * (1.0 / data.shape[0])
    centered = (data - mean).astype(jnp.bfloat16)
    centered_ref[...] = centered
    sketch = jnp.dot(turned[...], centered, preferred_element_type=jnp.float32).T

    @pl.when(i < steps)
    def _():
        mine_ref[...] = sketch

    @pl.when(i >= steps)
    def _():
        given_ref[...] = sketch


def center_and_sketch(side, shapes, signs):
    subjects, coords = shapes.shape
    width = signs.shape[1]
    half = coords // 2
    tile = math.gcd(half, 512)
    steps = half // tile

    def column(i, side):
        kept = i < steps
        return jnp.where(kept, side[0] * steps + i, (1 - side[0]) * steps + i - steps)

    return pl.pallas_call(
        functools.partial(sketch_kernel, steps),
        grid_spec=pltpu.PrefetchScalarGridSpec(
            num_scalar_prefetch=1,
            grid=(2 * steps,),
            in_specs=[
                pl.BlockSpec((subjects, tile), lambda i, side: (0, column(i, side))),
                pl.BlockSpec((subjects, width), lambda i, side: (0, 0)),
            ],
            out_specs=(
                pl.BlockSpec((subjects, tile), lambda i, side: (0, column(i, side))),
                pl.BlockSpec((tile, width), lambda i, side: (jnp.minimum(i, steps - 1), 0)),
                pl.BlockSpec((tile, width), lambda i, side: (jnp.maximum(i - steps, 0), 0)),
            ),
            scratch_shapes=[pltpu.VMEM((width, subjects), jnp.bfloat16)],
        ),
        out_shape=(
            jax.ShapeDtypeStruct((subjects, coords), jnp.bfloat16),
            jax.ShapeDtypeStruct((half, width), jnp.float32),
            jax.ShapeDtypeStruct((half, width), jnp.float32),
        ),
        name="center_and_sketch",
    )(side.reshape(1), shapes, signs)


def times_t(a, b):
    return lax.dot_general(a, b, (((1,), (1,)), ((), ())), precision=HIGHEST)


def mix(own, own_map, other, other_map):
    return jnp.matmul(own, own_map, precision=HIGHEST) + jnp.matmul(
        other, other_map, precision=HIGHEST
    )


def swap(value, distance):
    size = lax.axis_size("cohort")
    return lax.ppermute(value, "cohort", [(i, i ^ distance) for i in range(size)])


def on_device(shapes, sketch_signs, merge_sketch):
    n = lax.axis_size("coord")
    position = lax.axis_index("cohort")
    side = position % 2
    upper = position // 2 % 2
    centered, mine, given = center_and_sketch(side, shapes[0], sketch_signs[0])

    theirs = swap(given, 1)
    own_map = mixing_map(gram_sum((mine, given), n, False, 0), merge_sketch[0][side])
    mine = mix(mine, own_map, theirs, swap(own_map, 1))

    theirs = swap(mine, 2)
    own_map = mixing_map(gram_sum((mine,), n, True, 1), merge_sketch[1][upper])
    mine = mix(mine, own_map, theirs, swap(own_map, 2))

    mine = times_t(mine, lower_inverse(gram_sum((mine,), n, True, 2)))
    width = mine.shape[1]
    total_coords = shapes.shape[2] * n
    basis, scores = basis_and_scores(
        centered, mine, n, 4.0 * math.sqrt(width / total_coords), 3
    )
    return (basis * math.sqrt(total_coords))[None], scores[None]


def solution(mesh):
    placed = (P("cohort", None, "coord"), P("cohort", None, None), P())
    return jax.shard_map(
        on_device,
        mesh=mesh,
        in_specs=placed,
        out_specs=(P("cohort", "coord", None), P("cohort", "coord", None)),
        check_vma=False,
    )
```

```python
import functools
import math

import jax
import jax.numpy as jnp
from jax import lax
from jax.experimental import pallas as pl
from jax.experimental.pallas import tpu as pltpu
from jax.sharding import PartitionSpec as P

LEVELS = 2
HIGHEST = lax.Precision.HIGHEST
MESH = pl.DeviceIdType.MESH
VMEM = pl.BlockSpec(memory_space=pltpu.VMEM)


def peers_of(n, pair):
    coord = lax.axis_index("coord")
    if not pair:
        return coord, n, lambda rank: {"coord": rank}
    cohort = lax.axis_index("cohort")
    side = lax.rem(cohort, 2)
    base = cohort - side
    rank = coord * 2 + side
    return rank, 2 * n, lambda r: {"coord": r // 2, "cohort": base + lax.rem(r, 2)}


def greet(me, size, ident):
    barrier = pltpu.get_barrier_semaphore()
    for d in range(1, size):
        pl.semaphore_signal(
            barrier, inc=1, device_id=ident(lax.rem(me + d, size)), device_id_type=MESH
        )
    return barrier


def send_block(part_ref, recv, me, size, ident, send, got, d):
    peer = lax.rem(me + d, size)
    return pltpu.make_async_remote_copy(
        src_ref=part_ref.at[peer],
        dst_ref=recv.at[d],
        send_sem=send.at[d],
        recv_sem=got.at[d],
        device_id=ident(peer),
        device_id_type=MESH,
    )


def gram_sum_kernel(n, pair, count, *refs):
    rows_refs, (out_ref, gram, cross, part, recv, send, got, send2, got2) = refs[:count], refs[count:]
    me, size, ident = peers_of(n, pair)
    barrier = greet(me, size, ident)
    block = part.shape[1]
    width = gram.shape[0]
    gram[...] = jnp.zeros_like(gram)
    cross[...] = jnp.zeros_like(cross)

    def product(a, b):
        return lax.dot_general(
            a, b, (((0,), (0,)), ((), ())), preferred_element_type=jnp.float32
        )

    for rows_ref in rows_refs:
        step = math.gcd(rows_ref.shape[0], 512)

        def add(i, carry, rows_ref=rows_ref, step=step):
            rows = rows_ref[pl.ds(pl.multiple_of(i * step, step), step), :]
            high = rows.astype(jnp.bfloat16)
            rest = rows - high.astype(jnp.float32)
            middle = rest.astype(jnp.bfloat16)
            low = (rest - middle.astype(jnp.float32)).astype(jnp.bfloat16)
            wide = product(high, jnp.concatenate([high, middle], axis=1))
            gram[...] += wide[:, :width] + product(middle, middle)
            cross[...] += wide[:, width:] + product(high, low)
            return carry

        lax.fori_loop(0, rows_ref.shape[0] // step, add, 0)
    turned = cross[...]
    gram[...] += turned + turned.T
    for r in range(size):
        part[r] = gram[r * block : (r + 1) * block, :]
    pl.semaphore_wait(barrier, size - 1)
    copies = [send_block(part, recv, me, size, ident, send, got, d) for d in range(1, size)]
    for copy in copies:
        copy.start()
    total = part[me]
    for d in range(1, size):
        copies[d - 1].wait_recv()
        total = total + recv[d]
    out_ref[me] = total
    spread = []
    for d in range(1, size):
        spread.append(
            pltpu.make_async_remote_copy(
                src_ref=out_ref.at[me],
                dst_ref=out_ref.at[me],
                send_sem=send2.at[d],
                recv_sem=got2.at[d],
                device_id=ident(lax.rem(me + d, size)),
                device_id_type=MESH,
            )
        )
    for copy in spread:
        copy.start()
    for copy in spread:
        copy.wait_recv()
    for copy in copies + spread:
        copy.wait_send()


def gram_sum(parts, n, pair, ident):
    size = 2 * n if pair else n
    width = parts[0].shape[1]
    dtype = parts[0].dtype
    shape = (size, width // size, width)
    out = pl.pallas_call(
        functools.partial(gram_sum_kernel, n, pair, len(parts)),
        out_shape=jax.ShapeDtypeStruct(shape, dtype),
        in_specs=[VMEM] * len(parts),
        out_specs=VMEM,
        scratch_shapes=[
            pltpu.VMEM((width, width), dtype),
            pltpu.VMEM((width, width), dtype),
            pltpu.VMEM(shape, dtype),
            pltpu.VMEM(shape, dtype),
        ]
        + [pltpu.SemaphoreType.DMA((size,))] * 4,
        compiler_params=pltpu.CompilerParams(collective_id=ident, has_side_effects=True),
        name=f"gram_sum_{ident}",
    )(*parts)
    return out.reshape(width, width)


def score_kernel(
    n, scale, grow, centered_ref, own_ref, basis_ref, out_ref,
    held, narrow, part, recv, loaded, send, got, swap_send, swap_got,
):
    me, size, ident = peers_of(n, False)
    cohort = lax.axis_index("cohort")
    side = lax.rem(cohort, 2)
    partner = {"cohort": cohort + 1 - 2 * side}
    rows, half = held.shape[2:]
    order = [lax.rem(me + d, size) for d in list(range(1, size)) + [0]]
    loads = []
    for peer in order:
        pair = []
        for h in range(2):
            pair.append(
                pltpu.make_async_copy(
                    centered_ref.at[
                        pl.ds(pl.multiple_of(peer * rows, rows), rows), pl.ds(h * half, half)
                    ],
                    held.at[peer, h],
                    loaded.at[peer, h],
                )
            )
        loads.append(pair)
        for copy in pair:
            copy.start()
    barrier = greet(me, size, ident)
    pl.semaphore_signal(barrier, inc=1, device_id=partner, device_id_type=MESH)
    basis_ref[side] = own_ref[...]
    narrow[...] = own_ref[...].astype(jnp.bfloat16)
    pl.semaphore_wait(barrier, size)
    cross = pltpu.make_async_remote_copy(
        src_ref=own_ref,
        dst_ref=basis_ref.at[side],
        send_sem=swap_send,
        recv_sem=swap_got,
        device_id=partner,
        device_id_type=MESH,
    )
    cross.start()
    for peer, pair in zip(order, loads):
        for copy in pair:
            copy.wait()
        part[peer] = jnp.dot(held[peer, side], narrow[...], preferred_element_type=jnp.float32)
    cross.wait_recv()
    narrow[...] = basis_ref[1 - side].astype(jnp.bfloat16)
    copies = []
    for d, peer in zip(list(range(1, size)) + [0], order):
        part[peer] = part[peer] + jnp.dot(
            held[peer, 1 - side], narrow[...], preferred_element_type=jnp.float32
        )
        if d:
            copies.append(send_block(part, recv, me, size, ident, send, got, d))
            copies[-1].start()
    basis_ref[...] = basis_ref[...] * grow
    total = part[me]
    for d in range(1, size):
        copies[d - 1].wait_recv()
        total = total + recv[d]
    out_ref[...] = total * scale
    cross.wait_send()
    for copy in copies:
        copy.wait_send()


def basis_and_scores(centered, own, n, scale, grow, ident):
    subjects = centered.shape[0]
    half, width = own.shape
    rows = subjects // n
    blocks = (n, rows, width)
    basis, scores = pl.pallas_call(
        functools.partial(score_kernel, n, scale, grow),
        out_shape=(
            jax.ShapeDtypeStruct((2, half, width), own.dtype),
            jax.ShapeDtypeStruct((rows, width), jnp.float32),
        ),
        in_specs=[pl.BlockSpec(memory_space=pl.ANY), VMEM],
        out_specs=(VMEM, VMEM),
        scratch_shapes=[
            pltpu.VMEM((n, 2, rows, half), centered.dtype),
            pltpu.VMEM((half, width), jnp.bfloat16),
            pltpu.VMEM(blocks, jnp.float32),
            pltpu.VMEM(blocks, jnp.float32),
            pltpu.SemaphoreType.DMA((n, 2)),
            pltpu.SemaphoreType.DMA((n,)),
            pltpu.SemaphoreType.DMA((n,)),
            pltpu.SemaphoreType.DMA,
            pltpu.SemaphoreType.DMA,
        ],
        compiler_params=pltpu.CompilerParams(collective_id=ident, has_side_effects=True),
        name="basis_and_scores",
    )(centered, own)
    return basis.reshape(2 * half, width), scores


def inverse_of(g_ref, x_ref):
    size = g_ref.shape[0]
    step = 8
    tiles = size // step
    lane = lax.broadcasted_iota(jnp.int32, (step, size), 1)
    sub = lax.broadcasted_iota(jnp.int32, (step, size), 0)

    def full(x):
        return jnp.broadcast_to(x, (step, size))

    def total(terms):
        while len(terms) > 1:
            terms = [terms[i] + terms[i + 1] for i in range(0, len(terms), 2)]
        return terms[0]

    left = [g_ref[t * step : (t + 1) * step, :] for t in range(tiles)]
    right = [(lane == sub + t * step).astype(jnp.float32) for t in range(tiles)]
    for t in range(tiles):
        at = t * step
        cols = [full(left[t][:, at + k : at + k + 1]) for k in range(step)]
        e = [[full(cols[k][i : i + 1, :]) for k in range(i + 1)] for i in range(step)]
        rows = [full(left[t][i : i + 1, :]) for i in range(step)]
        rows_x = [full(right[t][i : i + 1, :]) for i in range(step)]
        f = {}
        inv = []
        for s in range(step):
            inv.append(1.0 / e[s][s])
            for i in range(s + 1, step):
                f[i, s] = e[i][s] * inv[s]
                for k in range(s + 1, i + 1):
                    e[i][k] = e[i][k] - f[i, s] * e[k][s]
            for i in range(s + 1, step):
                rows[i] = rows[i] - f[i, s] * rows[s]
                rows_x[i] = rows_x[i] - f[i, s] * rows_x[s]
        out = rows_x[0] * lax.rsqrt(e[0][0])
        for s in range(1, step):
            out = jnp.where(sub == s, rows_x[s] * lax.rsqrt(e[s][s]), out)
        x_ref[at : at + step, :] = out
        rows = [rows[s] * inv[s] for s in range(step)]
        rows_x = [rows_x[s] * inv[s] for s in range(step)]
        for u in range(t + 1, tiles):
            c = [full(left[u][:, at + s : at + s + 1]) for s in range(step)]
            for s in range(step):
                for r in range(s):
                    c[s] = c[s] - f[s, r] * c[r]
            left[u] = left[u] - total([c[s] * rows[s] for s in range(step)])
            right[u] = right[u] - total([c[s] * rows_x[s] for s in range(step)])


def map_kernel(g_ref, mix_ref, out_ref, x_ref):
    inverse_of(g_ref, x_ref)
    out_ref[...] = lax.dot_general(
        x_ref[...],
        mix_ref[...],
        (((0,), (0,)), ((), ())),
        precision=HIGHEST,
        preferred_element_type=jnp.float32,
    )


def lower_inverse(gram):
    return pl.pallas_call(
        inverse_of,
        out_shape=jax.ShapeDtypeStruct(gram.shape, gram.dtype),
        in_specs=[VMEM],
        out_specs=VMEM,
        name="lower_inverse",
    )(gram)


def mixing_map(gram, mix):
    return pl.pallas_call(
        map_kernel,
        out_shape=jax.ShapeDtypeStruct(gram.shape, gram.dtype),
        in_specs=[VMEM, VMEM],
        out_specs=VMEM,
        scratch_shapes=[pltpu.VMEM(gram.shape, gram.dtype)],
        name="mixing_map",
    )(gram, mix)


def sketch_kernel(steps, side_ref, shapes_ref, signs_ref, centered_ref, mine_ref, given_ref, turned):
    i = pl.program_id(0)

    @pl.when(i == 0)
    def _():
        turned[...] = signs_ref[...].astype(jnp.float32).T.astype(jnp.bfloat16)

    data = shapes_ref[...].astype(jnp.float32)
    mean = jnp.sum(data, axis=0, keepdims=True) * (1.0 / data.shape[0])
    centered = (data - mean).astype(jnp.bfloat16)
    centered_ref[...] = centered
    sketch = jnp.dot(turned[...], centered, preferred_element_type=jnp.float32).T

    @pl.when(i < steps)
    def _():
        mine_ref[...] = sketch

    @pl.when(i >= steps)
    def _():
        given_ref[...] = sketch


def center_and_sketch(side, shapes, signs):
    subjects, coords = shapes.shape
    width = signs.shape[1]
    half = coords // 2
    tile = math.gcd(half, 2048)
    steps = half // tile

    def column(i, side):
        kept = i < steps
        return jnp.where(kept, side[0] * steps + i, (1 - side[0]) * steps + i - steps)

    return pl.pallas_call(
        functools.partial(sketch_kernel, steps),
        grid_spec=pltpu.PrefetchScalarGridSpec(
            num_scalar_prefetch=1,
            grid=(2 * steps,),
            in_specs=[
                pl.BlockSpec((subjects, tile), lambda i, side: (0, column(i, side))),
                pl.BlockSpec((subjects, width), lambda i, side: (0, 0)),
            ],
            out_specs=(
                pl.BlockSpec((subjects, tile), lambda i, side: (0, column(i, side))),
                pl.BlockSpec((tile, width), lambda i, side: (jnp.minimum(i, steps - 1), 0)),
                pl.BlockSpec((tile, width), lambda i, side: (jnp.maximum(i - steps, 0), 0)),
            ),
            scratch_shapes=[pltpu.VMEM((width, subjects), jnp.bfloat16)],
        ),
        out_shape=(
            jax.ShapeDtypeStruct((subjects, coords), jnp.bfloat16),
            jax.ShapeDtypeStruct((half, width), jnp.float32),
            jax.ShapeDtypeStruct((half, width), jnp.float32),
        ),
        name="center_and_sketch",
    )(side.reshape(1), shapes, signs)


def times_t(a, b):
    return lax.dot_general(a, b, (((1,), (1,)), ((), ())), precision=HIGHEST)


def mix(own, own_map, other, other_map):
    return jnp.matmul(own, own_map, precision=HIGHEST) + jnp.matmul(
        other, other_map, precision=HIGHEST
    )


def swap(value, distance):
    size = lax.axis_size("cohort")
    return lax.ppermute(value, "cohort", [(i, i ^ distance) for i in range(size)])


def on_device(shapes, sketch_signs, merge_sketch):
    n = lax.axis_size("coord")
    position = lax.axis_index("cohort")
    side = position % 2
    upper = position // 2 % 2
    centered, mine, given = center_and_sketch(side, shapes[0], sketch_signs[0])

    theirs = swap(given, 1)
    own_map = mixing_map(gram_sum((mine, given), n, False, 0), merge_sketch[0][side])
    mine = mix(mine, own_map, theirs, swap(own_map, 1))

    theirs = swap(mine, 2)
    own_map = mixing_map(gram_sum((mine,), n, True, 1), merge_sketch[1][upper])
    mine = mix(mine, own_map, theirs, swap(own_map, 2))

    mine = times_t(mine, lower_inverse(gram_sum((mine,), n, True, 2)))
    width = mine.shape[1]
    total_coords = shapes.shape[2] * n
    basis, scores = basis_and_scores(
        centered, mine, n, 4.0 * math.sqrt(width / total_coords), math.sqrt(total_coords), 3
    )
    return basis[None], scores[None]


def solution(mesh):
    placed = (P("cohort", None, "coord"), P("cohort", None, None), P())
    return jax.shard_map(
        on_device,
        mesh=mesh,
        in_specs=placed,
        out_specs=(P("cohort", "coord", None), P("cohort", "coord", None)),
        check_vma=False,
    )
```
